32 devices in a mesh: parts: 2 (over x), harm: 4 (over y, core), tile: 4 (over z).
Axes of the slice: x: 2, y: 2, z: 4, core: 2. Of those that a mesh axis runs over, the one named last changes fastest.
Arguments:
- perturbation: float32 [8, 2, 5, 128, 256], P('harm', None, None, ('parts', 'tile')), parts along dimension 3, may hold values from -6 to 6
- base_flow: float32 [8, 2, 3, 128, 256], P('harm', None, None, ('parts', 'tile')), parts along dimension 3, may hold values from -0.9 to 0.9
- viscosity: float32 [128, 256], P(('parts', 'tile')), parts along dimension 0, may hold values from 0.05 to 0.5
Outputs:
- resolvent_image: float32 [8, 2, 5, 128, 256], P('harm', None, None, ('parts', 'tile')), parts along dimension 3
The draws below stay inside these ranges and needn't reach their ends.
There are 2 independent parts, one for each index of `parts`. The reference program is written for one: setup_inputs(seed, part) draws one part's arguments, and reference() takes and returns one part's arrays. A program takes and returns all parts, laid end to end along the dimension named above; each array names one. Nothing has to cross between parts.
All inputs are finite; a program needn't handle non-finite values.
Results may differ from the reference program's by a relative error of at most 0.00002.
Values sent between devices are 32-bit elements; how exact they have to be, the bound alone decides.
A program may use at most 64 MiB of HBM per device.

```python
import math
import jax
import jax.numpy as jnp
from jax import lax

FIELDS = 5
CY = 256
NH = 8
NXG = 64


def shard_levels(stream_key, dims, split, smallest, high):
    level, own = 1.0, jax.random.fold_in(stream_key, 6)
    for axis_at, parts in split:
        steps = jnp.exp(jax.random.uniform(jax.random.fold_in(own, axis_at), (parts,), jnp.float32, smallest / len(split), high / len(split)))
        level = level * jnp.repeat(steps, dims[axis_at] // parts).reshape([-1 if axis == axis_at else 1 for axis in range(len(dims))])
    return level


def scatter_about(own_key, dims, width, limit, shards=(), kind=jnp.bfloat16):
    drawn = width * jax.random.normal(own_key, dims, jnp.float32)
    if shards:
        drawn = drawn * shard_levels(own_key, dims, shards, -0.22, 0.18)
    return jnp.clip(drawn, -limit, limit).astype(kind)


def setup_inputs(seed: int = 0, part: int = 0) -> dict:
    streams_of = jax.random.split(jax.random.key(seed), 4)
    part_keys = jax.random.split(jax.random.fold_in(streams_of[3], part), 4)
    return {
        "perturbation": scatter_about(part_keys[0], (NH, 2, FIELDS, NXG, CY), 1.0, 6.0, ((0, 4), (3, 4)), jnp.float32),
        "base_flow": scatter_about(part_keys[1], (NH, 2, 3, NXG, CY), 0.15, 0.9, ((0, 4), (3, 4)), jnp.float32),
        "viscosity": jnp.clip(jnp.exp(math.log(0.5) - 2.3025851 * jax.random.uniform(part_keys[2], (NXG, CY), jnp.float32) ** shard_levels(part_keys[2], (NXG, CY), ((0, 4),), -0.2, 0.2)), 0.05, 0.5),
    }


omega_base = 0.25


def along_first(values):
    return 0.5 * (jnp.roll(values, -1, -2) - jnp.roll(values, 1, -2))


def along_second(values):
    return 0.5 * (jnp.roll(values, -1, -1) - jnp.roll(values, 1, -1))


def diffusion(values, viscosity):
    east_face = 0.5 * (viscosity + jnp.roll(viscosity, -1, -2))
    west_face = 0.5 * (viscosity + jnp.roll(viscosity, 1, -2))
    north_face = 0.5 * (viscosity + jnp.roll(viscosity, -1, -1))
    south_face = 0.5 * (viscosity + jnp.roll(viscosity, 1, -1))
    return (east_face * (jnp.roll(values, -1, -2) - values) - west_face * (values - jnp.roll(values, 1, -2))
            + north_face * (jnp.roll(values, -1, -1) - values) - south_face * (values - jnp.roll(values, 1, -1)))


def acoustic(grad_x, grad_y):
    dilation = grad_x[..., 1, :, :] + grad_y[..., 2, :, :]
    return jnp.stack([dilation, grad_x[..., 4, :, :], grad_y[..., 4, :, :], jnp.zeros_like(dilation), dilation], axis=-3)


def own_terms(middle, grad_x, grad_y, damping, frequency):
    rotation = jnp.stack([-frequency * middle[:, 1], frequency * middle[:, 0]], axis=1)
    return rotation + acoustic(grad_x, grad_y) - damping


def coupling(u_real, u_imag, v_real, v_imag, g_real, g_imag, q_real, q_imag, x_real, x_imag, y_real, y_imag):
    real_part = u_real * x_real - u_imag * x_imag + v_real * y_real - v_imag * y_imag + g_real * q_real - g_imag * q_imag
    imag_part = u_real * x_imag + u_imag * x_real + v_real * y_imag + v_imag * y_real + g_real * q_imag + g_imag * q_real
    return real_part, imag_part


def reference(perturbation, base_flow, viscosity):
    grad_x = along_first(perturbation)
    grad_y = along_second(perturbation)
    numbers = jnp.arange(NH, dtype=jnp.int32)
    signed = jnp.where(numbers < NH // 2, numbers, numbers - NH)
    frequency = (omega_base * signed.astype(jnp.float32)).reshape(NH, 1, 1, 1)
    summed = own_terms(perturbation, grad_x, grad_y, diffusion(perturbation, viscosity), frequency)

    def add_source(source, summed):
        shifted = jnp.roll(base_flow, source, axis=0)
        values = lax.dynamic_index_in_dim(perturbation, source, 0, keepdims=False)
        slope_x = lax.dynamic_index_in_dim(grad_x, source, 0, keepdims=False)
        slope_y = lax.dynamic_index_in_dim(grad_y, source, 0, keepdims=False)
        real_part, imag_part = coupling(
            shifted[:, 0, 0][:, None], shifted[:, 1, 0][:, None],
            shifted[:, 0, 1][:, None], shifted[:, 1, 1][:, None],
            shifted[:, 0, 2][:, None], shifted[:, 1, 2][:, None],
            values[0], values[1], slope_x[0], slope_x[1], slope_y[0], slope_y[1])
        return summed + jnp.stack([real_part, imag_part], axis=1)

    summed = lax.fori_loop(0, NH, add_source, summed)
    return summed
```

```python
import functools

import jax
import jax.numpy as jnp
from jax import lax
from jax.experimental import pallas as pl
from jax.experimental.pallas import tpu as pltpu
from jax.sharding import PartitionSpec as P

omega_base = 0.25
MESH = pl.DeviceIdType.MESH


def kernel(
    groups,
    tiles,
    p_hbm,
    b_hbm,
    v_hbm,
    out,
    pbuf,
    bbuf,
    vbuf,
    stage,
    rims,
    gx,
    gy,
    local_sem,
    y_send,
    y_recv,
    chip_send,
    chip_recv,
    z_send,
    z_recv,
    rim_send,
    rim_recv,
):
    local, _, fields, rows, width = p_hbm.shape
    total = pbuf.shape[0]
    cores = 2
    chips = groups // cores
    rim_rows = local * 2 * fields
    me = lax.axis_index("harm")
    chip, core = me // cores, me % cores
    place = lax.axis_index("tile")
    partner = chip * cores + (1 - core)
    above, below = (place + 1) % tiles, (place + tiles - 1) % tiles

    def group_at(distance, own_core):
        at = (chip + chips - distance) % chips
        return at * cores + (core if own_core else 1 - core)

    def target_at(distance):
        return (chip + distance) % chips * cores + core

    first = me * local

    copy_p = pltpu.make_async_copy(p_hbm, pbuf.at[pl.ds(first, local)], local_sem.at[0])
    copy_b = pltpu.make_async_copy(b_hbm, bbuf.at[pl.ds(first, local)], local_sem.at[1])
    copy_v = pltpu.make_async_copy(v_hbm, vbuf, local_sem.at[2])
    copy_p.start()
    copy_v.start()
    copy_b.start()

    barrier = pltpu.get_barrier_semaphore()
    for distance in range(1, chips):
        pl.semaphore_signal(
            barrier, inc=1, device_id={"harm": target_at(distance)}, device_id_type=MESH
        )
    pl.semaphore_signal(barrier, inc=1, device_id={"harm": partner}, device_id_type=MESH)
    pl.semaphore_signal(barrier, inc=1, device_id={"tile": above}, device_id_type=MESH)
    pl.semaphore_signal(barrier, inc=1, device_id={"tile": below}, device_id_type=MESH)

    def pack(distance):
        start = group_at(distance, True) * local
        for index in range(local):
            for part in range(2):
                for field in range(fields):
                    row = (index * 2 + part) * fields + field
                    stage[distance, 0, row : row + 1, :] = pbuf[start + index, part, field, 0:1, :]
                    stage[distance, 1, row : row + 1, :] = pbuf[
                        start + index, part, field, rows - 1 : rows, :
                    ]

    copy_p.wait()
    copy_v.wait()
    pack(0)
    stage[0, 0, rim_rows : rim_rows + 1, :] = vbuf[0:1, :]
    stage[0, 1, rim_rows : rim_rows + 1, :] = vbuf[rows - 1 : rows, :]

    pl.semaphore_wait(barrier, chips + 2)

    y_copies = []
    for kind in range(2):
        source, dest = ((p_hbm, pbuf), (b_hbm, bbuf))[kind]
        for index in range(local):
            for distance in range(1, chips):
                copy = pltpu.make_async_remote_copy(
                    src_ref=source.at[index],
                    dst_ref=dest.at[first + index],
                    send_sem=y_send.at[distance - 1, kind, index],
                    recv_sem=y_recv.at[distance - 1, kind, index],
                    device_id={"harm": target_at(distance)},
                    device_id_type=MESH,
                )
                copy.start()
                y_copies.append((distance, kind, index, copy))

    def rim_copies(distance):
        group = group_at(distance, True)
        return [
            pltpu.make_async_remote_copy(
                src_ref=stage.at[distance, side],
                dst_ref=rims.at[group, 1 - side],
                send_sem=z_send.at[distance, side],
                recv_sem=z_recv.at[distance, side],
                device_id={"tile": (below, above)[side]},
                device_id_type=MESH,
            )
            for side in range(2)
        ]

    started = []
    rim_pending = {}

    def send_rims(distance):
        rim_pending[distance] = rim_copies(distance)
        for copy in rim_pending[distance]:
            copy.start()

    def relay_copy(distance, kind, index):
        at = group_at(distance, True) * local + index
        dest = (pbuf, bbuf)[kind]
        source = dest.at[at] if distance else (p_hbm, b_hbm)[kind].at[index]
        return pltpu.make_async_remote_copy(
            src_ref=source,
            dst_ref=dest.at[at],
            send_sem=chip_send.at[distance, kind, index],
            recv_sem=chip_recv.at[distance, kind, index],
            device_id={"harm": partner},
            device_id_type=MESH,
        )

    relays = {}

    def relay(distance, kind, index):
        relays[distance, kind, index] = relay_copy(distance, kind, index)
        relays[distance, kind, index].start()

    def relay_rims(distance):
        group = group_at(distance, True)
        relays[distance] = pltpu.make_async_remote_copy(
            src_ref=rims.at[group],
            dst_ref=rims.at[group],
            send_sem=rim_send.at[distance],
            recv_sem=rim_recv.at[distance],
            device_id={"harm": partner},
            device_id_type=MESH,
        )
        relays[distance].start()

    send_rims(0)
    for kind in range(2):
        for index in range(local):
            relay(0, kind, index)

    row_at = lax.broadcasted_iota(jnp.int32, (rows, width), 0)

    def neighbours(value, low, high):
        east = jnp.where(row_at == rows - 1, high, pltpu.roll(value, rows - 1, 0))
        west = jnp.where(row_at == 0, low, pltpu.roll(value, 1, 0))
        return east, west

    def slope_y(group):
        def one(index, _):
            at = group * local + index
            for part in range(2):
                for field in range(fields):
                    value = pbuf[at, part, field]
                    gy[at, part, field] = 0.5 * (
                        pltpu.roll(value, width - 1, 1) - pltpu.roll(value, 1, 1)
                    )
            return 0

        lax.fori_loop(0, local, one, 0)

    def slope_x(group):
        for index in range(local):
            at = group * local + index
            for part in range(2):
                for field in range(fields):
                    row = (index * 2 + part) * fields + field
                    east, west = neighbours(
                        pbuf[at, part, field],
                        rims[group, 0, row : row + 1, :],
                        rims[group, 1, row : row + 1, :],
                    )
                    gx[at, part, field] = 0.5 * (east - west)

    def own_terms():
        center = vbuf[...]
        east, west = neighbours(
            center,
            rims[me, 0, rim_rows : rim_rows + 1, :],
            rims[me, 1, rim_rows : rim_rows + 1, :],
        )
        east_face = 0.5 * (center + east)
        west_face = 0.5 * (center + west)
        north_face = 0.5 * (center + pltpu.roll(center, width - 1, 1))
        south_face = 0.5 * (center + pltpu.roll(center, 1, 1))
        for index in range(local):
            at = first + index
            signed = jnp.where(at < total // 2, at, at - total)
            frequency = omega_base * signed.astype(jnp.float32)
            for part in range(2):
                for field in range(fields):
                    row = (index * 2 + part) * fields + field
                    value = pbuf[at, part, field]
                    up, down = neighbours(
                        value,
                        rims[me, 0, row : row + 1, :],
                        rims[me, 1, row : row + 1, :],
                    )
                    damping = (
                        east_face * (up - value)
                        - west_face * (value - down)
                        + north_face * (pltpu.roll(value, width - 1, 1) - value)
                        - south_face * (value - pltpu.roll(value, 1, 1))
                    )
                    turned = pbuf[at, 1 - part, field] * frequency
                    result = turned - damping if part else -turned - damping
                    if field == 0 or field == 4:
                        result = result + (gx[at, part, 1] + gy[at, part, 2])
                    elif field == 1:
                        result = result + gx[at, part, 4]
                    elif field == 2:
                        result = result + gy[at, part, 4]
                    out[index, part, field] = result

    def couple(at):
        def strip(step, _):
            span = pl.ds(pl.multiple_of(step * 8, 8), 8)
            base = [[bbuf[at, part, which, span, :] for part in range(2)] for which in range(3)]
            for index in range(local):
                source = (first + index + total - at) % total
                for field in range(fields):
                    real = out[index, 0, field, span, :]
                    imag = out[index, 1, field, span, :]
                    for which, values in ((0, gx), (1, gy), (2, pbuf)):
                        a_real, a_imag = base[which]
                        q_real = values[source, 0, field, span, :]
                        q_imag = values[source, 1, field, span, :]
                        real = real + a_real * q_real - a_imag * q_imag
                        imag = imag + a_real * q_imag + a_imag * q_real
                    out[index, 0, field, span, :] = real
                    out[index, 1, field, span, :] = imag
            return 0

        lax.fori_loop(0, rows // 8, strip, 0)

    def wait_y(distance, kind, index):
        for other, what, which, copy in y_copies:
            if (other, what, which) == (distance, kind, index):
                copy.wait_recv()

    slope_y(me)
    for copy in rim_pending[0]:
        copy.wait_recv()
    relay_rims(0)
    slope_x(me)
    own_terms()
    for index in range(local):
        relays[0, 0, index].wait_recv()
    slope_y(partner)
    relays[0].wait_recv()
    slope_x(partner)

    for distance in range(1, chips):
        for index in range(local):
            wait_y(distance, 0, index)
            relay(distance, 0, index)
        pack(distance)
        send_rims(distance)
    for distance in range(1, chips):
        slope_y(group_at(distance, True))
        for index in range(local):
            relays[distance, 0, index].wait_recv()
        slope_y(group_at(distance, False))
    for distance in range(1, chips):
        for index in range(local - 1):
            wait_y(distance, 1, index)
            relay(distance, 1, index)
    for distance in range(1, chips):
        for copy in rim_pending[distance]:
            copy.wait_recv()
        relay_rims(distance)
        slope_x(group_at(distance, True))
    for distance in range(1, chips):
        relays[distance].wait_recv()
        slope_x(group_at(distance, False))

    copy_b.wait()
    for index in range(local):
        couple(first + index)
    for index in range(local):
        relays[0, 1, index].wait_recv()
        couple(partner * local + index)
    for distance in range(1, chips):
        wait_y(distance, 1, local - 1)
        relay(distance, 1, local - 1)
    for distance in range(1, chips):
        for index in range(local):
            couple(group_at(distance, True) * local + index)
    for distance in range(1, chips):
        for index in range(local):
            relays[distance, 1, index].wait_recv()
            couple(group_at(distance, False) * local + index)

    for _, _, _, copy in y_copies:
        copy.wait_send()
    for copies in rim_pending.values():
        for copy in copies:
            copy.wait_send()
    for copy in relays.values():
        copy.wait_send()


def shards(perturbation, base_flow, viscosity):
    local, parts, fields, rows, width = perturbation.shape
    groups = lax.axis_size("harm")
    tiles = lax.axis_size("tile")
    chips = groups // 2
    total = local * groups
    rim = -(-(local * parts * fields + 1) // 8) * 8
    kinds = base_flow.shape[2]
    dma = pltpu.SemaphoreType.DMA
    f32 = jnp.float32
    return pl.pallas_call(
        functools.partial(kernel, groups, tiles),
        out_shape=jax.ShapeDtypeStruct(perturbation.shape, f32),
        in_specs=[pl.BlockSpec(memory_space=pl.ANY)] * 3,
        out_specs=pl.BlockSpec(memory_space=pltpu.VMEM),
        scratch_shapes=[
            pltpu.VMEM((total, 2, fields, rows, width), f32),
            pltpu.VMEM((total, 2, kinds, rows, width), f32),
            pltpu.VMEM((rows, width), f32),
            pltpu.VMEM((chips, 2, rim, width), f32),
            pltpu.VMEM((groups, 2, rim, width), f32),
            pltpu.VMEM((total, 2, fields, rows, width), f32),
            pltpu.VMEM((total, 2, fields, rows, width), f32),
            dma((3,)),
            dma((chips - 1, 2, local)),
            dma((chips - 1, 2, local)),
            dma((chips, 2, local)),
            dma((chips, 2, local)),
            dma((chips, 2)),
            dma((chips, 2)),
            dma((chips,)),
            dma((chips,)),
        ],
        compiler_params=pltpu.CompilerParams(collective_id=0, has_side_effects=True),
    )(perturbation, base_flow, viscosity)


def solution(mesh):
    placed = (
        P("harm", None, None, ("parts", "tile"), None),
        P("harm", None, None, ("parts", "tile"), None),
        P(("parts", "tile"), None),
    )
    return jax.shard_map(
        shards,
        mesh=mesh,
        in_specs=placed,
        out_specs=P("harm", None, None, ("parts", "tile"), None),
        check_vma=False,
    )
```

```python
import functools

import jax
import jax.numpy as jnp
from jax import lax
from jax.experimental import pallas as pl
from jax.experimental.pallas import tpu as pltpu
from jax.sharding import PartitionSpec as P

omega_base = 0.25
MESH = pl.DeviceIdType.MESH


def kernel(
    groups,
    tiles,
    p_hbm,
    b_hbm,
    v_hbm,
    out,
    pbuf,
    bbuf,
    vbuf,
    stage,
    rims,
    gx,
    gy,
    local_sem,
    y_send,
    y_recv,
    chip_send,
    chip_recv,
    z_send,
    z_recv,
    rim_send,
    rim_recv,
):
    local, _, fields, rows, width = p_hbm.shape
    total = pbuf.shape[0]
    cores = 2
    chips = groups // cores
    rim_rows = local * 2 * fields
    me = lax.axis_index("harm")
    chip, core = me // cores, me % cores
    place = lax.axis_index("tile")
    partner = chip * cores + (1 - core)
    above, below = (place + 1) % tiles, (place + tiles - 1) % tiles

    def group_at(distance, own_core):
        at = (chip + chips - distance) % chips
        return at * cores + (core if own_core else 1 - core)

    def target_at(distance):
        return (chip + distance) % chips * cores + core

    first = me * local

    copy_p = pltpu.make_async_copy(p_hbm, pbuf.at[pl.ds(first, local)], local_sem.at[0])
    copy_b = pltpu.make_async_copy(b_hbm, bbuf.at[pl.ds(first, local)], local_sem.at[1])
    copy_v = pltpu.make_async_copy(v_hbm, vbuf, local_sem.at[2])
    copy_p.start()
    copy_v.start()
    copy_b.start()

    barrier = pltpu.get_barrier_semaphore()
    for distance in range(1, chips):
        pl.semaphore_signal(
            barrier, inc=1, device_id={"harm": target_at(distance)}, device_id_type=MESH
        )
    pl.semaphore_signal(barrier, inc=1, device_id={"harm": partner}, device_id_type=MESH)
    pl.semaphore_signal(barrier, inc=1, device_id={"tile": above}, device_id_type=MESH)
    pl.semaphore_signal(barrier, inc=1, device_id={"tile": below}, device_id_type=MESH)

    def pack(distance):
        start = group_at(distance, True) * local
        for index in range(local):
            for part in range(2):
                for field in range(fields):
                    row = (index * 2 + part) * fields + field
                    stage[distance, 0, row : row + 1, :] = pbuf[start + index, part, field, 0:1, :]
                    stage[distance, 1, row : row + 1, :] = pbuf[
                        start + index, part, field, rows - 1 : rows, :
                    ]

    copy_p.wait()
    copy_v.wait()
    pack(0)
    stage[0, 0, rim_rows : rim_rows + 1, :] = vbuf[0:1, :]
    stage[0, 1, rim_rows : rim_rows + 1, :] = vbuf[rows - 1 : rows, :]

    pl.semaphore_wait(barrier, chips + 2)

    y_copies = []
    for kind in range(2):
        source, dest = ((p_hbm, pbuf), (b_hbm, bbuf))[kind]
        for index in range(local):
            for distance in range(1, chips):
                copy = pltpu.make_async_remote_copy(
                    src_ref=source.at[index],
                    dst_ref=dest.at[first + index],
                    send_sem=y_send.at[distance - 1, kind, index],
                    recv_sem=y_recv.at[distance - 1, kind, index],
                    device_id={"harm": target_at(distance)},
                    device_id_type=MESH,
                )
                copy.start()
                y_copies.append((distance, kind, index, copy))

    def rim_copies(distance):
        group = group_at(distance, True)
        return [
            pltpu.make_async_remote_copy(
                src_ref=stage.at[distance, side],
                dst_ref=rims.at[group, 1 - side],
                send_sem=z_send.at[distance, side],
                recv_sem=z_recv.at[distance, side],
                device_id={"tile": (below, above)[side]},
                device_id_type=MESH,
            )
            for side in range(2)
        ]

    started = []
    rim_pending = {}

    def send_rims(distance):
        rim_pending[distance] = rim_copies(distance)
        for copy in rim_pending[distance]:
            copy.start()

    def relay_copy(distance, kind, index):
        at = group_at(distance, True) * local + index
        dest = (pbuf, bbuf)[kind]
        source = dest.at[at] if distance else (p_hbm, b_hbm)[kind].at[index]
        return pltpu.make_async_remote_copy(
            src_ref=source,
            dst_ref=dest.at[at],
            send_sem=chip_send.at[distance, kind, index],
            recv_sem=chip_recv.at[distance, kind, index],
            device_id={"harm": partner},
            device_id_type=MESH,
        )

    relays = {}

    def relay(distance, kind, index):
        relays[distance, kind, index] = relay_copy(distance, kind, index)
        relays[distance, kind, index].start()

    def relay_rims(distance):
        group = group_at(distance, True)
        relays[distance] = pltpu.make_async_remote_copy(
            src_ref=rims.at[group],
            dst_ref=rims.at[group],
            send_sem=rim_send.at[distance],
            recv_sem=rim_recv.at[distance],
            device_id={"harm": partner},
            device_id_type=MESH,
        )
        relays[distance].start()

    send_rims(0)
    for kind in range(2):
        for index in range(local):
            relay(0, kind, index)

    row_at = lax.broadcasted_iota(jnp.int32, (rows, width), 0)

    def neighbours(value, low, high):
        east = jnp.where(row_at == rows - 1, high, pltpu.roll(value, rows - 1, 0))
        west = jnp.where(row_at == 0, low, pltpu.roll(value, 1, 0))
        return east, west

    def slope_y(group):
        def one(index, _):
            at = group * local + index
            for part in range(2):
                for field in range(fields):
                    value = pbuf[at, part, field]
                    gy[at, part, field] = 0.5 * (
                        pltpu.roll(value, width - 1, 1) - pltpu.roll(value, 1, 1)
                    )
            return 0

        lax.fori_loop(0, local, one, 0)

    def slope_x(group):
        for index in range(local):
            at = group * local + index
            for part in range(2):
                for field in range(fields):
                    row = (index * 2 + part) * fields + field
                    east, west = neighbours(
                        pbuf[at, part, field],
                        rims[group, 0, row : row + 1, :],
                        rims[group, 1, row : row + 1, :],
                    )
                    gx[at, part, field] = 0.5 * (east - west)

    def own_terms():
        center = vbuf[...]
        east, west = neighbours(
            center,
            rims[me, 0, rim_rows : rim_rows + 1, :],
            rims[me, 1, rim_rows : rim_rows + 1, :],
        )
        east_face = 0.5 * (center + east)
        west_face = 0.5 * (center + west)
        north_face = 0.5 * (center + pltpu.roll(center, width - 1, 1))
        south_face = 0.5 * (center + pltpu.roll(center, 1, 1))
        for index in range(local):
            at = first + index
            signed = jnp.where(at < total // 2, at, at - total)
            frequency = omega_base * signed.astype(jnp.float32)
            for part in range(2):
                for field in range(fields):
                    row = (index * 2 + part) * fields + field
                    value = pbuf[at, part, field]
                    up, down = neighbours(
                        value,
                        rims[me, 0, row : row + 1, :],
                        rims[me, 1, row : row + 1, :],
                    )
                    damping = (
                        east_face * (up - value)
                        - west_face * (value - down)
                        + north_face * (pltpu.roll(value, width - 1, 1) - value)
                        - south_face * (value - pltpu.roll(value, 1, 1))
                    )
                    turned = pbuf[at, 1 - part, field] * frequency
                    result = turned - damping if part else -turned - damping
                    if field == 0 or field == 4:
                        result = result + (gx[at, part, 1] + gy[at, part, 2])
                    elif field == 1:
                        result = result + gx[at, part, 4]
                    elif field == 2:
                        result = result + gy[at, part, 4]
                    out[index, part, field] = result

    def couple(at):
        def strip(step, _):
            span = pl.ds(pl.multiple_of(step * 8, 8), 8)
            base = [[bbuf[at, part, which, span, :] for part in range(2)] for which in range(3)]
            for index in range(local):
                source = (first + index + total - at) % total
                for field in range(fields):
                    real = out[index, 0, field, span, :]
                    imag = out[index, 1, field, span, :]
                    for which, values in ((0, gx), (1, gy), (2, pbuf)):
                        a_real, a_imag = base[which]
                        q_real = values[source, 0, field, span, :]
                        q_imag = values[source, 1, field, span, :]
                        real = real + a_real * q_real - a_imag * q_imag
                        imag = imag + a_real * q_imag + a_imag * q_real
                    out[index, 0, field, span, :] = real
                    out[index, 1, field, span, :] = imag
            return 0

        lax.fori_loop(0, rows // 8, strip, 0)

    def wait_y(distance, kind, index):
        for other, what, which, copy in y_copies:
            if (other, what, which) == (distance, kind, index):
                copy.wait_recv()

    slope_y(me)
    for copy in rim_pending[0]:
        copy.wait_recv()
    relay_rims(0)
    slope_x(me)
    own_terms()
    for index in range(local):
        relays[0, 0, index].wait_recv()
    slope_y(partner)
    relays[0].wait_recv()
    slope_x(partner)

    for distance in range(1, chips):
        for index in range(local):
            wait_y(distance, 0, index)
            relay(distance, 0, index)
        pack(distance)
        send_rims(distance)
    for distance in range(1, chips):
        slope_y(group_at(distance, True))
        for index in range(local):
            relays[distance, 0, index].wait_recv()
        slope_y(group_at(distance, False))
    for distance in range(1, chips):
        for index in range(local - 1):
            wait_y(distance, 1, index)
            relay(distance, 1, index)
    for distance in range(1, chips):
        for copy in rim_pending[distance]:
            copy.wait_recv()
        relay_rims(distance)
        slope_x(group_at(distance, True))
    for distance in range(1, chips):
        relays[distance].wait_recv()
        slope_x(group_at(distance, False))

    copy_b.wait()
    for index in range(local):
        couple(first + index)
    for index in range(local):
        relays[0, 1, index].wait_recv()
        couple(partner * local + index)
    for distance in range(1, chips):
        wait_y(distance, 1, local - 1)
        relay(distance, 1, local - 1)
    for distance in range(1, chips):
        for index in range(local):
            couple(group_at(distance, True) * local + index)
    for distance in range(1, chips):
        for index in range(local):
            relays[distance, 1, index].wait_recv()
            couple(group_at(distance, False) * local + index)

    for _, _, _, copy in y_copies:
        copy.wait_send()
    for copies in rim_pending.values():
        for copy in copies:
            copy.wait_send()
    for copy in relays.values():
        copy.wait_send()


def shards(perturbation, base_flow, viscosity):
    local, parts, fields, rows, width = perturbation.shape
    groups = lax.axis_size("harm")
    tiles = lax.axis_size("tile")
    chips = groups // 2
    if chips == 2 and rows % 16 == 0:
        return halves(perturbation, base_flow, viscosity)
    total = local * groups
    rim = -(-(local * parts * fields + 1) // 8) * 8
    kinds = base_flow.shape[2]
    dma = pltpu.SemaphoreType.DMA
    f32 = jnp.float32
    return pl.pallas_call(
        functools.partial(kernel, groups, tiles),
        out_shape=jax.ShapeDtypeStruct(perturbation.shape, f32),
        in_specs=[pl.BlockSpec(memory_space=pl.ANY)] * 3,
        out_specs=pl.BlockSpec(memory_space=pltpu.VMEM),
        scratch_shapes=[
            pltpu.VMEM((total, 2, fields, rows, width), f32),
            pltpu.VMEM((total, 2, kinds, rows, width), f32),
            pltpu.VMEM((rows, width), f32),
            pltpu.VMEM((chips, 2, rim, width), f32),
            pltpu.VMEM((groups, 2, rim, width), f32),
            pltpu.VMEM((total, 2, fields, rows, width), f32),
            pltpu.VMEM((total, 2, fields, rows, width), f32),
            dma((3,)),
            dma((chips - 1, 2, local)),
            dma((chips - 1, 2, local)),
            dma((chips, 2, local)),
            dma((chips, 2, local)),
            dma((chips, 2)),
            dma((chips, 2)),
            dma((chips,)),
            dma((chips,)),
        ],
        compiler_params=pltpu.CompilerParams(collective_id=0, has_side_effects=True),
    )(perturbation, base_flow, viscosity)


def half_kernel(
    groups,
    tiles,
    p_hbm,
    b_hbm,
    v_hbm,
    out_hbm,
    full,
    phalf,
    bhalf,
    vbuf,
    stage,
    inner,
    zrims,
    edges,
    gx,
    gy,
    total,
    sent,
    back,
    local_sem,
    out_sem,
    y_send,
    y_recv,
    chip_send,
    chip_recv,
    z_send,
    z_recv,
    up_token,
    down_token,
):
    local, _, fields, rows, width = p_hbm.shape
    harmonics = phalf.shape[0]
    half = rows // 2
    rim_rows = local * 2 * fields
    me = lax.axis_index("harm")
    chip, core = me // 2, me % 2
    place = lax.axis_index("tile")
    partner = chip * 2 + (1 - core)
    across = (1 - chip) * 2 + core
    corner = (1 - chip) * 2 + (1 - core)
    above, below = (place + 1) % tiles, (place + tiles - 1) % tiles
    first = me * local
    mine = pl.ds(pl.multiple_of(chip * half, 8), half)
    theirs = pl.ds(pl.multiple_of((1 - chip) * half, 8), half)

    def at_group(ref, group):
        return ref.at[pl.ds(group * local, local)]

    loads = [
        pltpu.make_async_copy(source, dest, local_sem.at[at])
        for at, (source, dest) in enumerate(
            (
                (p_hbm, full),
                (v_hbm, vbuf),
                (p_hbm.at[:, :, :, mine, :], at_group(phalf, me)),
                (b_hbm.at[:, :, :, mine, :], at_group(bhalf, me)),
            )
        )
    ]
    for copy in loads:
        copy.start()

    barrier = pltpu.get_barrier_semaphore()
    pl.semaphore_signal(barrier, inc=1, device_id={"harm": across}, device_id_type=MESH)
    pl.semaphore_signal(barrier, inc=1, device_id={"harm": partner}, device_id_type=MESH)

    @pl.when(place < tiles - 1)
    def _():
        pl.semaphore_signal(barrier, inc=1, device_id={"tile": above}, device_id_type=MESH)

    @pl.when(place > 0)
    def _():
        pl.semaphore_signal(barrier, inc=1, device_id={"tile": below}, device_id_type=MESH)

    in_line = (place < tiles - 1).astype(jnp.int32) + (place > 0).astype(jnp.int32)

    loads[0].wait()
    loads[1].wait()
    for index in range(local):
        for part in range(2):
            for field in range(fields):
                row = (index * 2 + part) * fields + field
                span = slice(row, row + 1)
                stage[0, span, :] = full[index, part, field, 0:1, :]
                stage[1, span, :] = full[index, part, field, rows - 1 : rows, :]
                edges[me, chip, span, :] = full[index, part, field, pl.ds(half - chip, 1), :]
                inner[span, :] = full[index, part, field, pl.ds(half - 1 + chip, 1), :]
    stage[0, rim_rows : rim_rows + 1, :] = vbuf[0:1, :]
    stage[1, rim_rows : rim_rows + 1, :] = vbuf[rows - 1 : rows, :]

    pl.semaphore_wait(barrier, 2 + in_line)

    started = []

    def remote(source, dest, send, recv, at, **device):
        copy = pltpu.make_async_remote_copy(
            src_ref=source,
            dst_ref=dest,
            send_sem=send.at[at],
            recv_sem=recv.at[at],
            device_id=device,
            device_id_type=MESH,
        )
        copy.start()
        started.append(copy)
        return copy

    def over_y(source, dest, at):
        return remote(source, dest, y_send, y_recv, at, harm=across)

    def on_chip(source, dest, at):
        return remote(source, dest, chip_send, chip_recv, at, harm=partner)

    def send_field(field):
        return over_y(
            p_hbm.at[:, :, field, theirs, :], at_group(phalf, me).at[:, :, field], 3 + field
        )

    early = min(3, fields)
    y_base = over_y(b_hbm.at[:, :, :, theirs, :], at_group(bhalf, me), 0)
    y_field = [send_field(field) for field in range(early)]
    c_base = on_chip(b_hbm.at[:, :, :, mine, :], at_group(bhalf, me), 0)
    c_own = on_chip(p_hbm.at[:, :, :, mine, :], at_group(phalf, me), 1)

    if tiles > 2:

        @pl.when(place >= 2)
        def _():
            pl.semaphore_wait(up_token, 1)

        @pl.when((place >= 1) & (place < tiles - 1))
        def _():
            pl.semaphore_signal(up_token, inc=1, device_id={"tile": above}, device_id_type=MESH)

        @pl.when(place <= tiles - 3)
        def _():
            pl.semaphore_wait(down_token, 1)

        @pl.when((place >= 1) & (place < tiles - 1))
        def _():
            pl.semaphore_signal(down_token, inc=1, device_id={"tile": below}, device_id_type=MESH)

    z_rims = [
        remote(stage.at[0], zrims.at[0], z_send, z_recv, 1, tile=below),
        remote(stage.at[1], zrims.at[1], z_send, z_recv, 0, tile=above),
    ]

    row_at = lax.broadcasted_iota(jnp.int32, (rows, width), 0)

    def neighbours(value, high, low):
        count = value.shape[0]
        row = row_at[:count]
        east = jnp.where(row == count - 1, high, pltpu.roll(value, count - 1, 0))
        west = jnp.where(row == 0, low, pltpu.roll(value, 1, 0))
        return east, west

    def north(value):
        return pltpu.roll(value, width - 1, 1)

    def south(value):
        return pltpu.roll(value, 1, 1)

    def slopes(group, field):
        for index in range(local):
            at = group * local + index
            for part in range(2):
                row = (index * 2 + part) * fields + field
                value = phalf[at, part, field]
                east, west = neighbours(
                    value, edges[group, 0, row : row + 1, :], edges[group, 1, row : row + 1, :]
                )
                gx[at, part, field] = 0.5 * (east - west)
                gy[at, part, field] = 0.5 * (north(value) - south(value))

    def own_terms():
        center = vbuf[...]
        east, west = neighbours(
            center,
            zrims[0, rim_rows : rim_rows + 1, :],
            zrims[1, rim_rows : rim_rows + 1, :],
        )
        east_face = 0.5 * (center + east)
        west_face = 0.5 * (center + west)
        north_face = 0.5 * (center + north(center))
        south_face = 0.5 * (center + south(center))
        for index in range(local):
            at = first + index
            signed = jnp.where(at < harmonics // 2, at, at - harmonics)
            frequency = omega_base * signed.astype(jnp.float32)
            for part in range(2):

                def sides(field):
                    row = (index * 2 + part) * fields + field
                    return neighbours(
                        full[index, part, field],
                        zrims[0, row : row + 1, :],
                        zrims[1, row : row + 1, :],
                    )

                def along_x(field):
                    up, down = sides(field)
                    return 0.5 * (up - down)

                def along_y(field):
                    value = full[index, part, field]
                    return 0.5 * (north(value) - south(value))

                dilation = along_x(1) + along_y(2)
                sound = {0: dilation, 4: dilation, 1: along_x(4), 2: along_y(4)}
                for field in range(fields):
                    value = full[index, part, field]
                    up, down = sides(field)
                    damping = (
                        east_face * (up - value)
                        - west_face * (value - down)
                        + north_face * (north(value) - value)
                        - south_face * (value - south(value))
                    )
                    turned = full[index, 1 - part, field] * frequency
                    result = turned if part else -turned
                    if field in sound:
                        result = result + sound[field]
                    total[index, part, field] = result - damping

    z_rims[0].wait_recv()
    z_rims[1].wait_recv()
    y_outer = over_y(zrims.at[chip], edges.at[me, chip], 1)
    y_inner = over_y(inner, edges.at[me, 1 - chip], 2)
    y_field += [send_field(field) for field in range(early, fields)]
    edges[me, 1 - chip] = zrims[1 - chip]
    own_terms()
    c_edges = on_chip(edges.at[me], edges.at[me], 2)

    y_base.wait_recv()
    c_base_across = on_chip(at_group(bhalf, across), at_group(bhalf, across), 3)
    loads[2].wait()
    loads[3].wait()
    for field in range(fields):
        slopes(me, field)

    c_field = []

    def relay_field(field):
        y_field[field].wait_recv()
        c_field.append(
            on_chip(
                at_group(phalf, across).at[:, :, field],
                at_group(phalf, across).at[:, :, field],
                5 + field,
            )
        )

    for field in range(early):
        relay_field(field)
    c_own.wait_recv()
    c_edges.wait_recv()
    for field in range(fields):
        slopes(partner, field)
    y_outer.wait_recv()
    y_inner.wait_recv()
    c_edges_across = on_chip(edges.at[across], edges.at[across], 4)
    c_base.wait_recv()
    c_base_across.wait_recv()

    def couple(field):
        targets = [first + index for index in range(local)]
        targets += [across * local + index for index in range(local)]

        def step(source, sums):
            moved = [
                [values[source, part, field] for part in range(2)] for values in (gx, gy, phalf)
            ]
            after = []
            for number, target in enumerate(targets):
                real, imag = sums[2 * number], sums[2 * number + 1]
                at = (target + harmonics - source) % harmonics
                for which in range(3):
                    a_real, a_imag = bhalf[at, 0, which], bhalf[at, 1, which]
                    q_real, q_imag = moved[which]
                    real = real + a_real * q_real - a_imag * q_imag
                    imag = imag + a_real * q_imag + a_imag * q_real
                after += [real, imag]
            return tuple(after)

        zero = jnp.zeros((half, width), jnp.float32)
        sums = lax.fori_loop(0, harmonics, step, (zero,) * (4 * local), unroll=2)
        for index in range(local):
            for part in range(2):
                sent[index, part, field] = sums[2 * (local + index) + part]
        for index in range(local):
            for part in range(2):
                total[index, part, field, mine, :] += sums[2 * index + part]

    def put(field, span, which):
        copy = pltpu.make_async_copy(
            total.at[:, :, field, span, :],
            out_hbm.at[:, :, field, span, :],
            out_sem.at[which, field],
        )
        copy.start()
        puts.append(copy)

    puts = []
    y_back = []
    for field in range(fields):
        slopes(across, field)
        if field == 0:
            c_edges_across.wait_recv()
        c_field[field].wait_recv()
        slopes(corner, field)
        couple(field)
        y_back.append(over_y(sent.at[:, :, field], back.at[:, :, field], 3 + fields + field))
        put(field, mine, 0)
        if field + early < fields:
            relay_field(field + early)

    for field in range(fields):
        y_back[field].wait_recv()
        for index in range(local):
            for part in range(2):
                total[index, part, field, theirs, :] += back[index, part, field]
        put(field, theirs, 1)

    for copy in started:
        copy.wait_send()
    for copy in puts:
        copy.wait()


def halves(perturbation, base_flow, viscosity):
    local, _, fields, rows, width = perturbation.shape
    groups = lax.axis_size("harm")
    tiles = lax.axis_size("tile")
    harmonics = local * groups
    half = rows // 2
    rim = -(-(local * 2 * fields + 1) // 8) * 8
    kinds = base_flow.shape[2]
    dma = pltpu.SemaphoreType.DMA
    f32 = jnp.float32
    return pl.pallas_call(
        functools.partial(half_kernel, groups, tiles),
        out_shape=jax.ShapeDtypeStruct(perturbation.shape, f32),
        in_specs=[pl.BlockSpec(memory_space=pl.ANY)] * 3,
        out_specs=pl.BlockSpec(memory_space=pl.ANY),
        scratch_shapes=[
            pltpu.VMEM((local, 2, fields, rows, width), f32),
            pltpu.VMEM((harmonics, 2, fields, half, width), f32),
            pltpu.VMEM((harmonics, 2, kinds, half, width), f32),
            pltpu.VMEM((rows, width), f32),
            pltpu.VMEM((2, rim, width), f32),
            pltpu.VMEM((rim, width), f32),
            pltpu.VMEM((2, rim, width), f32),
            pltpu.VMEM((groups, 2, rim, width), f32),
            pltpu.VMEM((harmonics, 2, fields, half, width), f32),
            pltpu.VMEM((harmonics, 2, fields, half, width), f32),
            pltpu.VMEM((local, 2, fields, rows, width), f32),
            pltpu.VMEM((local, 2, fields, half, width), f32),
            pltpu.VMEM((local, 2, fields, half, width), f32),
            dma((4,)),
            dma((2, fields)),
            dma((3 + 2 * fields,)),
            dma((3 + 2 * fields,)),
            dma((5 + fields,)),
            dma((5 + fields,)),
            dma((2,)),
            dma((2,)),
            pltpu.SemaphoreType.REGULAR,
            pltpu.SemaphoreType.REGULAR,
        ],
        compiler_params=pltpu.CompilerParams(collective_id=0, has_side_effects=True),
    )(perturbation, base_flow, viscosity)


def solution(mesh):
    placed = (
        P("harm", None, None, ("parts", "tile"), None),
        P("harm", None, None, ("parts", "tile"), None),
        P(("parts", "tile"), None),
    )
    return jax.shard_map(
        shards,
        mesh=mesh,
        in_specs=placed,
        out_specs=P("harm", None, None, ("parts", "tile"), None),
        check_vma=False,
    )
```

```python
import functools

import jax
import jax.numpy as jnp
from jax import lax
from jax.experimental import pallas as pl
from jax.experimental.pallas import tpu as pltpu
from jax.sharding import PartitionSpec as P

omega_base = 0.25
MESH = pl.DeviceIdType.MESH


def kernel(
    groups,
    tiles,
    p_hbm,
    b_hbm,
    v_hbm,
    out,
    pbuf,
    bbuf,
    vbuf,
    stage,
    rims,
    gx,
    gy,
    local_sem,
    y_send,
    y_recv,
    chip_send,
    chip_recv,
    z_send,
    z_recv,
    rim_send,
    rim_recv,
):
    local, _, fields, rows, width = p_hbm.shape
    total = pbuf.shape[0]
    cores = 2
    chips = groups // cores
    rim_rows = local * 2 * fields
    me = lax.axis_index("harm")
    chip, core = me // cores, me % cores
    place = lax.axis_index("tile")
    partner = chip * cores + (1 - core)
    above, below = (place + 1) % tiles, (place + tiles - 1) % tiles

    def group_at(distance, own_core):
        at = (chip + chips - distance) % chips
        return at * cores + (core if own_core else 1 - core)

    def target_at(distance):
        return (chip + distance) % chips * cores + core

    first = me * local

    copy_p = pltpu.make_async_copy(p_hbm, pbuf.at[pl.ds(first, local)], local_sem.at[0])
    copy_b = pltpu.make_async_copy(b_hbm, bbuf.at[pl.ds(first, local)], local_sem.at[1])
    copy_v = pltpu.make_async_copy(v_hbm, vbuf, local_sem.at[2])
    copy_p.start()
    copy_v.start()
    copy_b.start()

    barrier = pltpu.get_barrier_semaphore()
    for distance in range(1, chips):
        pl.semaphore_signal(
            barrier, inc=1, device_id={"harm": target_at(distance)}, device_id_type=MESH
        )
    pl.semaphore_signal(barrier, inc=1, device_id={"harm": partner}, device_id_type=MESH)
    pl.semaphore_signal(barrier, inc=1, device_id={"tile": above}, device_id_type=MESH)
    pl.semaphore_signal(barrier, inc=1, device_id={"tile": below}, device_id_type=MESH)

    def pack(distance):
        start = group_at(distance, True) * local
        for index in range(local):
            for part in range(2):
                for field in range(fields):
                    row = (index * 2 + part) * fields + field
                    stage[distance, 0, row : row + 1, :] = pbuf[start + index, part, field, 0:1, :]
                    stage[distance, 1, row : row + 1, :] = pbuf[
                        start + index, part, field, rows - 1 : rows, :
                    ]

    copy_p.wait()
    copy_v.wait()
    pack(0)
    stage[0, 0, rim_rows : rim_rows + 1, :] = vbuf[0:1, :]
    stage[0, 1, rim_rows : rim_rows + 1, :] = vbuf[rows - 1 : rows, :]

    pl.semaphore_wait(barrier, chips + 2)

    y_copies = []
    for kind in range(2):
        source, dest = ((p_hbm, pbuf), (b_hbm, bbuf))[kind]
        for index in range(local):
            for distance in range(1, chips):
                copy = pltpu.make_async_remote_copy(
                    src_ref=source.at[index],
                    dst_ref=dest.at[first + index],
                    send_sem=y_send.at[distance - 1, kind, index],
                    recv_sem=y_recv.at[distance - 1, kind, index],
                    device_id={"harm": target_at(distance)},
                    device_id_type=MESH,
                )
                copy.start()
                y_copies.append((distance, kind, index, copy))

    def rim_copies(distance):
        group = group_at(distance, True)
        return [
            pltpu.make_async_remote_copy(
                src_ref=stage.at[distance, side],
                dst_ref=rims.at[group, 1 - side],
                send_sem=z_send.at[distance, side],
                recv_sem=z_recv.at[distance, side],
                device_id={"tile": (below, above)[side]},
                device_id_type=MESH,
            )
            for side in range(2)
        ]

    started = []
    rim_pending = {}

    def send_rims(distance):
        rim_pending[distance] = rim_copies(distance)
        for copy in rim_pending[distance]:
            copy.start()

    def relay_copy(distance, kind, index):
        at = group_at(distance, True) * local + index
        dest = (pbuf, bbuf)[kind]
        source = dest.at[at] if distance else (p_hbm, b_hbm)[kind].at[index]
        return pltpu.make_async_remote_copy(
            src_ref=source,
            dst_ref=dest.at[at],
            send_sem=chip_send.at[distance, kind, index],
            recv_sem=chip_recv.at[distance, kind, index],
            device_id={"harm": partner},
            device_id_type=MESH,
        )

    relays = {}

    def relay(distance, kind, index):
        relays[distance, kind, index] = relay_copy(distance, kind, index)
        relays[distance, kind, index].start()

    def relay_rims(distance):
        group = group_at(distance, True)
        relays[distance] = pltpu.make_async_remote_copy(
            src_ref=rims.at[group],
            dst_ref=rims.at[group],
            send_sem=rim_send.at[distance],
            recv_sem=rim_recv.at[distance],
            device_id={"harm": partner},
            device_id_type=MESH,
        )
        relays[distance].start()

    send_rims(0)
    for kind in range(2):
        for index in range(local):
            relay(0, kind, index)

    row_at = lax.broadcasted_iota(jnp.int32, (rows, width), 0)

    def neighbours(value, low, high):
        east = jnp.where(row_at == rows - 1, high, pltpu.roll(value, rows - 1, 0))
        west = jnp.where(row_at == 0, low, pltpu.roll(value, 1, 0))
        return east, west

    def slope_y(group):
        def one(index, _):
            at = group * local + index
            for part in range(2):
                for field in range(fields):
                    value = pbuf[at, part, field]
                    gy[at, part, field] = 0.5 * (
                        pltpu.roll(value, width - 1, 1) - pltpu.roll(value, 1, 1)
                    )
            return 0

        lax.fori_loop(0, local, one, 0)

    def slope_x(group):
        for index in range(local):
            at = group * local + index
            for part in range(2):
                for field in range(fields):
                    row = (index * 2 + part) * fields + field
                    east, west = neighbours(
                        pbuf[at, part, field],
                        rims[group, 0, row : row + 1, :],
                        rims[group, 1, row : row + 1, :],
                    )
                    gx[at, part, field] = 0.5 * (east - west)

    def own_terms():
        center = vbuf[...]
        east, west = neighbours(
            center,
            rims[me, 0, rim_rows : rim_rows + 1, :],
            rims[me, 1, rim_rows : rim_rows + 1, :],
        )
        east_face = 0.5 * (center + east)
        west_face = 0.5 * (center + west)
        north_face = 0.5 * (center + pltpu.roll(center, width - 1, 1))
        south_face = 0.5 * (center + pltpu.roll(center, 1, 1))
        for index in range(local):
            at = first + index
            signed = jnp.where(at < total // 2, at, at - total)
            frequency = omega_base * signed.astype(jnp.float32)
            for part in range(2):
                for field in range(fields):
                    row = (index * 2 + part) * fields + field
                    value = pbuf[at, part, field]
                    up, down = neighbours(
                        value,
                        rims[me, 0, row : row + 1, :],
                        rims[me, 1, row : row + 1, :],
                    )
                    damping = (
                        east_face * (up - value)
                        - west_face * (value - down)
                        + north_face * (pltpu.roll(value, width - 1, 1) - value)
                        - south_face * (value - pltpu.roll(value, 1, 1))
                    )
                    turned = pbuf[at, 1 - part, field] * frequency
                    result = turned - damping if part else -turned - damping
                    if field == 0 or field == 4:
                        result = result + (gx[at, part, 1] + gy[at, part, 2])
                    elif field == 1:
                        result = result + gx[at, part, 4]
                    elif field == 2:
                        result = result + gy[at, part, 4]
                    out[index, part, field] = result

    def couple(at):
        def strip(step, _):
            span = pl.ds(pl.multiple_of(step * 8, 8), 8)
            base = [[bbuf[at, part, which, span, :] for part in range(2)] for which in range(3)]
            for index in range(local):
                source = (first + index + total - at) % total
                for field in range(fields):
                    real = out[index, 0, field, span, :]
                    imag = out[index, 1, field, span, :]
                    for which, values in ((0, gx), (1, gy), (2, pbuf)):
                        a_real, a_imag = base[which]
                        q_real = values[source, 0, field, span, :]
                        q_imag = values[source, 1, field, span, :]
                        real = real + a_real * q_real - a_imag * q_imag
                        imag = imag + a_real * q_imag + a_imag * q_real
                    out[index, 0, field, span, :] = real
                    out[index, 1, field, span, :] = imag
            return 0

        lax.fori_loop(0, rows // 8, strip, 0)

    def wait_y(distance, kind, index):
        for other, what, which, copy in y_copies:
            if (other, what, which) == (distance, kind, index):
                copy.wait_recv()

    slope_y(me)
    for copy in rim_pending[0]:
        copy.wait_recv()
    relay_rims(0)
    slope_x(me)
    own_terms()
    for index in range(local):
        relays[0, 0, index].wait_recv()
    slope_y(partner)
    relays[0].wait_recv()
    slope_x(partner)

    for distance in range(1, chips):
        for index in range(local):
            wait_y(distance, 0, index)
            relay(distance, 0, index)
        pack(distance)
        send_rims(distance)
    for distance in range(1, chips):
        slope_y(group_at(distance, True))
        for index in range(local):
            relays[distance, 0, index].wait_recv()
        slope_y(group_at(distance, False))
    for distance in range(1, chips):
        for index in range(local - 1):
            wait_y(distance, 1, index)
            relay(distance, 1, index)
    for distance in range(1, chips):
        for copy in rim_pending[distance]:
            copy.wait_recv()
        relay_rims(distance)
        slope_x(group_at(distance, True))
    for distance in range(1, chips):
        relays[distance].wait_recv()
        slope_x(group_at(distance, False))

    copy_b.wait()
    for index in range(local):
        couple(first + index)
    for index in range(local):
        relays[0, 1, index].wait_recv()
        couple(partner * local + index)
    for distance in range(1, chips):
        wait_y(distance, 1, local - 1)
        relay(distance, 1, local - 1)
    for distance in range(1, chips):
        for index in range(local):
            couple(group_at(distance, True) * local + index)
    for distance in range(1, chips):
        for index in range(local):
            relays[distance, 1, index].wait_recv()
            couple(group_at(distance, False) * local + index)

    for _, _, _, copy in y_copies:
        copy.wait_send()
    for copies in rim_pending.values():
        for copy in copies:
            copy.wait_send()
    for copy in relays.values():
        copy.wait_send()


def shards(perturbation, base_flow, viscosity):
    local, parts, fields, rows, width = perturbation.shape
    groups = lax.axis_size("harm")
    tiles = lax.axis_size("tile")
    chips = groups // 2
    if chips == 2 and rows % 16 == 0:
        return halves(perturbation, base_flow, viscosity)
    total = local * groups
    rim = -(-(local * parts * fields + 1) // 8) * 8
    kinds = base_flow.shape[2]
    dma = pltpu.SemaphoreType.DMA
    f32 = jnp.float32
    return pl.pallas_call(
        functools.partial(kernel, groups, tiles),
        out_shape=jax.ShapeDtypeStruct(perturbation.shape, f32),
        in_specs=[pl.BlockSpec(memory_space=pl.ANY)] * 3,
        out_specs=pl.BlockSpec(memory_space=pltpu.VMEM),
        scratch_shapes=[
            pltpu.VMEM((total, 2, fields, rows, width), f32),
            pltpu.VMEM((total, 2, kinds, rows, width), f32),
            pltpu.VMEM((rows, width), f32),
            pltpu.VMEM((chips, 2, rim, width), f32),
            pltpu.VMEM((groups, 2, rim, width), f32),
            pltpu.VMEM((total, 2, fields, rows, width), f32),
            pltpu.VMEM((total, 2, fields, rows, width), f32),
            dma((3,)),
            dma((chips - 1, 2, local)),
            dma((chips - 1, 2, local)),
            dma((chips, 2, local)),
            dma((chips, 2, local)),
            dma((chips, 2)),
            dma((chips, 2)),
            dma((chips,)),
            dma((chips,)),
        ],
        compiler_params=pltpu.CompilerParams(collective_id=0, has_side_effects=True),
    )(perturbation, base_flow, viscosity)


def half_kernel(
    groups,
    tiles,
    p_hbm,
    b_hbm,
    v_hbm,
    out_hbm,
    full,
    phalf,
    bhalf,
    vbuf,
    stage,
    inner,
    zrims,
    edges,
    outer,
    fixes,
    fixed,
    kept,
    gx,
    gy,
    total,
    sent,
    back,
    local_sem,
    out_sem,
    y_send,
    y_recv,
    chip_send,
    chip_recv,
    z_send,
    z_recv,
    up_token,
    down_token,
):
    local, _, fields, rows, width = p_hbm.shape
    harmonics = phalf.shape[0]
    half = rows // 2
    rim_rows = local * 2 * fields
    rim = stage.shape[1]
    me = lax.axis_index("harm")
    chip, core = me // 2, me % 2
    place = lax.axis_index("tile")
    partner = chip * 2 + (1 - core)
    across = (1 - chip) * 2 + core
    corner = (1 - chip) * 2 + (1 - core)
    above, below = (place + 1) % tiles, (place + tiles - 1) % tiles
    first = me * local
    mine = pl.ds(pl.multiple_of(chip * half, 8), half)
    theirs = pl.ds(pl.multiple_of((1 - chip) * half, 8), half)

    def at_group(ref, group):
        return ref.at[pl.ds(group * local, local)]

    loads = [
        pltpu.make_async_copy(source, dest, local_sem.at[at])
        for at, (source, dest) in enumerate(
            (
                (p_hbm, full),
                (v_hbm, vbuf),
                (p_hbm.at[:, :, :, mine, :], at_group(phalf, me)),
                (b_hbm.at[:, :, :, mine, :], at_group(bhalf, me)),
            )
        )
    ]
    for copy in loads:
        copy.start()

    barrier = pltpu.get_barrier_semaphore()
    pl.semaphore_signal(barrier, inc=1, device_id={"harm": across}, device_id_type=MESH)
    pl.semaphore_signal(barrier, inc=1, device_id={"harm": partner}, device_id_type=MESH)

    @pl.when(place < tiles - 1)
    def _():
        pl.semaphore_signal(barrier, inc=1, device_id={"tile": above}, device_id_type=MESH)

    @pl.when(place > 0)
    def _():
        pl.semaphore_signal(barrier, inc=1, device_id={"tile": below}, device_id_type=MESH)

    in_line = (place < tiles - 1).astype(jnp.int32) + (place > 0).astype(jnp.int32)

    loads[0].wait()
    loads[1].wait()
    for index in range(local):
        for part in range(2):
            for field in range(fields):
                row = (index * 2 + part) * fields + field
                span = slice(row, row + 1)
                stage[0, span, :] = full[index, part, field, 0:1, :]
                stage[1, span, :] = full[index, part, field, rows - 1 : rows, :]
                edges[me, span, :] = full[index, part, field, pl.ds(half - chip, 1), :]
                inner[span, :] = full[index, part, field, pl.ds(half - 1 + chip, 1), :]
    stage[0, rim_rows : rim_rows + 1, :] = vbuf[0:1, :]
    stage[1, rim_rows : rim_rows + 1, :] = vbuf[rows - 1 : rows, :]

    pl.semaphore_wait(barrier, 2 + in_line)

    started = []

    def remote(source, dest, send, recv, at, **device):
        copy = pltpu.make_async_remote_copy(
            src_ref=source,
            dst_ref=dest,
            send_sem=send.at[at],
            recv_sem=recv.at[at],
            device_id=device,
            device_id_type=MESH,
        )
        copy.start()
        started.append(copy)
        return copy

    def over_y(source, dest, at):
        return remote(source, dest, y_send, y_recv, at, harm=across)

    def on_chip(source, dest, at):
        return remote(source, dest, chip_send, chip_recv, at, harm=partner)

    def send_field(field):
        return over_y(
            p_hbm.at[:, :, field, theirs, :], at_group(phalf, me).at[:, :, field], 3 + field
        )

    y_base = over_y(b_hbm.at[:, :, :, theirs, :], at_group(bhalf, me), 0)
    y_inner = over_y(inner, edges.at[me], 2)
    y_field = [send_field(field) for field in range(fields)]
    c_base = on_chip(b_hbm.at[:, :, :, mine, :], at_group(bhalf, me), 0)
    c_own = on_chip(p_hbm.at[:, :, :, mine, :], at_group(phalf, me), 1)
    c_edges = on_chip(edges.at[me], edges.at[me], 2)

    if tiles > 2:

        @pl.when(place >= 2)
        def _():
            pl.semaphore_wait(up_token, 1)

        @pl.when((place >= 1) & (place < tiles - 1))
        def _():
            pl.semaphore_signal(up_token, inc=1, device_id={"tile": above}, device_id_type=MESH)

        @pl.when(place <= tiles - 3)
        def _():
            pl.semaphore_wait(down_token, 1)

        @pl.when((place >= 1) & (place < tiles - 1))
        def _():
            pl.semaphore_signal(down_token, inc=1, device_id={"tile": below}, device_id_type=MESH)

    z_rims = [
        remote(stage.at[0], zrims.at[0], z_send, z_recv, 1, tile=below),
        remote(stage.at[1], zrims.at[1], z_send, z_recv, 0, tile=above),
    ]

    row_at = lax.broadcasted_iota(jnp.int32, (rows, width), 0)

    def neighbours(value, high, low):
        count = value.shape[0]
        row = row_at[:count]
        east = jnp.where(row == count - 1, high, pltpu.roll(value, count - 1, 0))
        west = jnp.where(row == 0, low, pltpu.roll(value, 1, 0))
        return east, west

    def north(value):
        return pltpu.roll(value, width - 1, 1)

    def south(value):
        return pltpu.roll(value, 1, 1)

    def slopes(group, field):
        for index in range(local):
            at = group * local + index
            for part in range(2):
                row = (index * 2 + part) * fields + field
                value = phalf[at, part, field]
                inside = edges[group, row : row + 1, :]
                east, west = neighbours(
                    value, inside * (1 - chip).astype(inside.dtype), inside * chip.astype(inside.dtype)
                )
                gx[at, part, field] = 0.5 * (east - west)
                gy[at, part, field] = 0.5 * (north(value) - south(value))

    def own_terms():
        center = vbuf[...]
        east, west = neighbours(
            center,
            zrims[0, rim_rows : rim_rows + 1, :],
            zrims[1, rim_rows : rim_rows + 1, :],
        )
        east_face = 0.5 * (center + east)
        west_face = 0.5 * (center + west)
        north_face = 0.5 * (center + north(center))
        south_face = 0.5 * (center + south(center))
        for index in range(local):
            at = first + index
            signed = jnp.where(at < harmonics // 2, at, at - harmonics)
            frequency = omega_base * signed.astype(jnp.float32)
            for part in range(2):

                def sides(field):
                    row = (index * 2 + part) * fields + field
                    return neighbours(
                        full[index, part, field],
                        zrims[0, row : row + 1, :],
                        zrims[1, row : row + 1, :],
                    )

                def along_x(field):
                    up, down = sides(field)
                    return 0.5 * (up - down)

                def along_y(field):
                    value = full[index, part, field]
                    return 0.5 * (north(value) - south(value))

                dilation = along_x(1) + along_y(2)
                sound = {0: dilation, 4: dilation, 1: along_x(4), 2: along_y(4)}
                for field in range(fields):
                    value = full[index, part, field]
                    up, down = sides(field)
                    damping = (
                        east_face * (up - value)
                        - west_face * (value - down)
                        + north_face * (north(value) - value)
                        - south_face * (value - south(value))
                    )
                    turned = full[index, 1 - part, field] * frequency
                    result = turned if part else -turned
                    if field in sound:
                        result = result + sound[field]
                    total[index, part, field] = result - damping

    y_base.wait_recv()
    c_base_across = on_chip(at_group(bhalf, across), at_group(bhalf, across), 3)
    loads[2].wait()
    loads[3].wait()
    for field in range(fields):
        slopes(me, field)

    c_field = []

    def relay_field(field):
        y_field[field].wait_recv()
        c_field.append(
            on_chip(
                at_group(phalf, across).at[:, :, field],
                at_group(phalf, across).at[:, :, field],
                5 + field,
            )
        )

    relay_field(0)
    c_own.wait_recv()
    c_edges.wait_recv()
    for field in range(fields):
        slopes(partner, field)
    y_inner.wait_recv()
    c_edges_across = on_chip(edges.at[across], edges.at[across], 4)
    c_base.wait_recv()
    c_base_across.wait_recv()
    if fields > 1:
        relay_field(1)

    targets = [first + index for index in range(local)]
    targets += [across * local + index for index in range(local)]

    def couple(field):
        def step(source, sums):
            moved = [
                [values[source, part, field] for part in range(2)] for values in (gx, gy, phalf)
            ]
            after = []
            for number, target in enumerate(targets):
                real, imag = sums[2 * number], sums[2 * number + 1]
                at = (target + harmonics - source) % harmonics
                for which in range(3):
                    a_real, a_imag = bhalf[at, 0, which], bhalf[at, 1, which]
                    q_real, q_imag = moved[which]
                    real = real + a_real * q_real - a_imag * q_imag
                    imag = imag + a_real * q_imag + a_imag * q_real
                after += [real, imag]
            return tuple(after)

        zero = jnp.zeros((half, width), jnp.float32)
        sums = lax.fori_loop(0, harmonics, step, (zero,) * (4 * local), unroll=2)
        for index in range(local):
            for part in range(2):
                sent[index, part, field] = sums[2 * (local + index) + part]
        for index in range(local):
            for part in range(2):
                kept[index, part, field] = sums[2 * index + part]

    def fix():
        edge = chip * (half - 1)
        sign = 0.5 * (2 * chip - 1).astype(jnp.float32)
        for number, target in enumerate(targets):
            real = jnp.zeros((fields, width), jnp.float32)
            imag = real
            for group in (me, partner, across, corner):
                for index in range(local):
                    at = (target + harmonics - group * local - index) % harmonics
                    a_real = sign * bhalf[at, 0, 0, pl.ds(edge, 1), :]
                    a_imag = sign * bhalf[at, 1, 0, pl.ds(edge, 1), :]
                    row = index * 2 * fields
                    q_real = outer[group, row : row + fields, :]
                    q_imag = outer[group, row + fields : row + 2 * fields, :]
                    real = real + a_real * q_real - a_imag * q_imag
                    imag = imag + a_real * q_imag + a_imag * q_real
            row = number // local * rim + number % local * 2 * fields
            fixes[row : row + fields, :] = real
            fixes[row + fields : row + 2 * fields, :] = imag

    def put(span, which):
        copy = pltpu.make_async_copy(
            total.at[:, :, :, span, :], out_hbm.at[:, :, :, span, :], out_sem.at[which]
        )
        copy.start()
        puts.append(copy)

    puts = []
    y_back = []
    for field in range(fields):
        slopes(across, field)
        if field == 0:
            c_edges_across.wait_recv()
        c_field[field].wait_recv()
        slopes(corner, field)
        couple(field)
        y_back.append(over_y(sent.at[:, :, field], back.at[:, :, field], 3 + fields + field))
        if field + 2 < fields:
            relay_field(field + 2)
        if field == 0:
            z_rims[0].wait_recv()
            z_rims[1].wait_recv()
            y_outer = over_y(zrims.at[chip], outer.at[me], 1)
            c_outer = on_chip(zrims.at[1 - chip], outer.at[me], 5 + fields)
            outer[me] = zrims[1 - chip]
            own_terms()
        if field == min(2, fields - 1):
            y_outer.wait_recv()
            c_outer_across = on_chip(outer.at[across], outer.at[across], 6 + fields)

    c_outer.wait_recv()
    c_outer_across.wait_recv()
    fix()
    y_fix = over_y(fixes.at[rim : 2 * rim], fixed, 3 + 2 * fields)

    def add_rows(rows_ref, at):
        for index in range(local):
            for part in range(2):
                for field in range(fields):
                    row = (index * 2 + part) * fields + field
                    total[index, part, field, pl.ds(at, 1), :] += rows_ref[row : row + 1, :]

    for field in range(fields):
        for index in range(local):
            for part in range(2):
                total[index, part, field, mine, :] += kept[index, part, field]
    add_rows(fixes, chip * (rows - 1))
    put(mine, 0)

    for field in range(fields):
        y_back[field].wait_recv()
        for index in range(local):
            for part in range(2):
                total[index, part, field, theirs, :] += back[index, part, field]
    y_fix.wait_recv()
    add_rows(fixed, (1 - chip) * (rows - 1))
    put(theirs, 1)

    for copy in started:
        copy.wait_send()
    for copy in puts:
        copy.wait()


def halves(perturbation, base_flow, viscosity):
    local, _, fields, rows, width = perturbation.shape
    groups = lax.axis_size("harm")
    tiles = lax.axis_size("tile")
    harmonics = local * groups
    half = rows // 2
    rim = -(-(local * 2 * fields + 1) // 8) * 8
    kinds = base_flow.shape[2]
    dma = pltpu.SemaphoreType.DMA
    f32 = jnp.float32
    return pl.pallas_call(
        functools.partial(half_kernel, groups, tiles),
        out_shape=jax.ShapeDtypeStruct(perturbation.shape, f32),
        in_specs=[pl.BlockSpec(memory_space=pl.ANY)] * 3,
        out_specs=pl.BlockSpec(memory_space=pl.ANY),
        scratch_shapes=[
            pltpu.VMEM((local, 2, fields, rows, width), f32),
            pltpu.VMEM((harmonics, 2, fields, half, width), f32),
            pltpu.VMEM((harmonics, 2, kinds, half, width), f32),
            pltpu.VMEM((rows, width), f32),
            pltpu.VMEM((2, rim, width), f32),
            pltpu.VMEM((rim, width), f32),
            pltpu.VMEM((2, rim, width), f32),
            pltpu.VMEM((groups, rim, width), f32),
            pltpu.VMEM((groups, rim, width), f32),
            pltpu.VMEM((2 * rim, width), f32),
            pltpu.VMEM((rim, width), f32),
            pltpu.VMEM((local, 2, fields, half, width), f32),
            pltpu.VMEM((harmonics, 2, fields, half, width), f32),
            pltpu.VMEM((harmonics, 2, fields, half, width), f32),
            pltpu.VMEM((local, 2, fields, rows, width), f32),
            pltpu.VMEM((local, 2, fields, half, width), f32),
            pltpu.VMEM((local, 2, fields, half, width), f32),
            dma((4,)),
            dma((2,)),
            dma((4 + 2 * fields,)),
            dma((4 + 2 * fields,)),
            dma((7 + fields,)),
            dma((7 + fields,)),
            dma((2,)),
            dma((2,)),
            pltpu.SemaphoreType.REGULAR,
            pltpu.SemaphoreType.REGULAR,
        ],
        compiler_params=pltpu.CompilerParams(collective_id=0, has_side_effects=True),
    )(perturbation, base_flow, viscosity)


def solution(mesh):
    placed = (
        P("harm", None, None, ("parts", "tile"), None),
        P("harm", None, None, ("parts", "tile"), None),
        P(("parts", "tile"), None),
    )
    return jax.shard_map(
        shards,
        mesh=mesh,
        in_specs=placed,
        out_specs=P("harm", None, None, ("parts", "tile"), None),
        check_vma=False,
    )
```

```python
import functools

import jax
import jax.numpy as jnp
from jax import lax
from jax.experimental import pallas as pl
from jax.experimental.pallas import tpu as pltpu
from jax.sharding import PartitionSpec as P

omega_base = 0.25
MESH = pl.DeviceIdType.MESH


def kernel(
    groups,
    tiles,
    p_hbm,
    b_hbm,
    v_hbm,
    out,
    pbuf,
    bbuf,
    vbuf,
    stage,
    rims,
    gx,
    gy,
    local_sem,
    y_send,
    y_recv,
    chip_send,
    chip_recv,
    z_send,
    z_recv,
    rim_send,
    rim_recv,
):
    local, _, fields, rows, width = p_hbm.shape
    total = pbuf.shape[0]
    cores = 2
    chips = groups // cores
    rim_rows = local * 2 * fields
    me = lax.axis_index("harm")
    chip, core = me // cores, me % cores
    place = lax.axis_index("tile")
    partner = chip * cores + (1 - core)
    above, below = (place + 1) % tiles, (place + tiles - 1) % tiles

    def group_at(distance, own_core):
        at = (chip + chips - distance) % chips
        return at * cores + (core if own_core else 1 - core)

    def target_at(distance):
        return (chip + distance) % chips * cores + core

    first = me * local

    copy_p = pltpu.make_async_copy(p_hbm, pbuf.at[pl.ds(first, local)], local_sem.at[0])
    copy_b = pltpu.make_async_copy(b_hbm, bbuf.at[pl.ds(first, local)], local_sem.at[1])
    copy_v = pltpu.make_async_copy(v_hbm, vbuf, local_sem.at[2])
    copy_p.start()
    copy_v.start()
    copy_b.start()

    barrier = pltpu.get_barrier_semaphore()
    for distance in range(1, chips):
        pl.semaphore_signal(
            barrier, inc=1, device_id={"harm": target_at(distance)}, device_id_type=MESH
        )
    pl.semaphore_signal(barrier, inc=1, device_id={"harm": partner}, device_id_type=MESH)
    pl.semaphore_signal(barrier, inc=1, device_id={"tile": above}, device_id_type=MESH)
    pl.semaphore_signal(barrier, inc=1, device_id={"tile": below}, device_id_type=MESH)

    def pack(distance):
        start = group_at(distance, True) * local
        for index in range(local):
            for part in range(2):
                for field in range(fields):
                    row = (index * 2 + part) * fields + field
                    stage[distance, 0, row : row + 1, :] = pbuf[start + index, part, field, 0:1, :]
                    stage[distance, 1, row : row + 1, :] = pbuf[
                        start + index, part, field, rows - 1 : rows, :
                    ]

    copy_p.wait()
    copy_v.wait()
    pack(0)
    stage[0, 0, rim_rows : rim_rows + 1, :] = vbuf[0:1, :]
    stage[0, 1, rim_rows : rim_rows + 1, :] = vbuf[rows - 1 : rows, :]

    pl.semaphore_wait(barrier, chips + 2)

    y_copies = []
    for kind in range(2):
        source, dest = ((p_hbm, pbuf), (b_hbm, bbuf))[kind]
        for index in range(local):
            for distance in range(1, chips):
                copy = pltpu.make_async_remote_copy(
                    src_ref=source.at[index],
                    dst_ref=dest.at[first + index],
                    send_sem=y_send.at[distance - 1, kind, index],
                    recv_sem=y_recv.at[distance - 1, kind, index],
                    device_id={"harm": target_at(distance)},
                    device_id_type=MESH,
                )
                copy.start()
                y_copies.append((distance, kind, index, copy))

    def rim_copies(distance):
        group = group_at(distance, True)
        return [
            pltpu.make_async_remote_copy(
                src_ref=stage.at[distance, side],
                dst_ref=rims.at[group, 1 - side],
                send_sem=z_send.at[distance, side],
                recv_sem=z_recv.at[distance, side],
                device_id={"tile": (below, above)[side]},
                device_id_type=MESH,
            )
            for side in range(2)
        ]

    started = []
    rim_pending = {}

    def send_rims(distance):
        rim_pending[distance] = rim_copies(distance)
        for copy in rim_pending[distance]:
            copy.start()

    def relay_copy(distance, kind, index):
        at = group_at(distance, True) * local + index
        dest = (pbuf, bbuf)[kind]
        source = dest.at[at] if distance else (p_hbm, b_hbm)[kind].at[index]
        return pltpu.make_async_remote_copy(
            src_ref=source,
            dst_ref=dest.at[at],
            send_sem=chip_send.at[distance, kind, index],
            recv_sem=chip_recv.at[distance, kind, index],
            device_id={"harm": partner},
            device_id_type=MESH,
        )

    relays = {}

    def relay(distance, kind, index):
        relays[distance, kind, index] = relay_copy(distance, kind, index)
        relays[distance, kind, index].start()

    def relay_rims(distance):
        group = group_at(distance, True)
        relays[distance] = pltpu.make_async_remote_copy(
            src_ref=rims.at[group],
            dst_ref=rims.at[group],
            send_sem=rim_send.at[distance],
            recv_sem=rim_recv.at[distance],
            device_id={"harm": partner},
            device_id_type=MESH,
        )
        relays[distance].start()

    send_rims(0)
    for kind in range(2):
        for index in range(local):
            relay(0, kind, index)

    row_at = lax.broadcasted_iota(jnp.int32, (rows, width), 0)

    def neighbours(value, low, high):
        east = jnp.where(row_at == rows - 1, high, pltpu.roll(value, rows - 1, 0))
        west = jnp.where(row_at == 0, low, pltpu.roll(value, 1, 0))
        return east, west

    def slope_y(group):
        def one(index, _):
            at = group * local + index
            for part in range(2):
                for field in range(fields):
                    value = pbuf[at, part, field]
                    gy[at, part, field] = 0.5 * (
                        pltpu.roll(value, width - 1, 1) - pltpu.roll(value, 1, 1)
                    )
            return 0

        lax.fori_loop(0, local, one, 0)

    def slope_x(group):
        for index in range(local):
            at = group * local + index
            for part in range(2):
                for field in range(fields):
                    row = (index * 2 + part) * fields + field
                    east, west = neighbours(
                        pbuf[at, part, field],
                        rims[group, 0, row : row + 1, :],
                        rims[group, 1, row : row + 1, :],
                    )
                    gx[at, part, field] = 0.5 * (east - west)

    def own_terms():
        center = vbuf[...]
        east, west = neighbours(
            center,
            rims[me, 0, rim_rows : rim_rows + 1, :],
            rims[me, 1, rim_rows : rim_rows + 1, :],
        )
        east_face = 0.5 * (center + east)
        west_face = 0.5 * (center + west)
        north_face = 0.5 * (center + pltpu.roll(center, width - 1, 1))
        south_face = 0.5 * (center + pltpu.roll(center, 1, 1))
        for index in range(local):
            at = first + index
            signed = jnp.where(at < total // 2, at, at - total)
            frequency = omega_base * signed.astype(jnp.float32)
            for part in range(2):
                for field in range(fields):
                    row = (index * 2 + part) * fields + field
                    value = pbuf[at, part, field]
                    up, down = neighbours(
                        value,
                        rims[me, 0, row : row + 1, :],
                        rims[me, 1, row : row + 1, :],
                    )
                    damping = (
                        east_face * (up - value)
                        - west_face * (value - down)
                        + north_face * (pltpu.roll(value, width - 1, 1) - value)
                        - south_face * (value - pltpu.roll(value, 1, 1))
                    )
                    turned = pbuf[at, 1 - part, field] * frequency
                    result = turned - damping if part else -turned - damping
                    if field == 0 or field == 4:
                        result = result + (gx[at, part, 1] + gy[at, part, 2])
                    elif field == 1:
                        result = result + gx[at, part, 4]
                    elif field == 2:
                        result = result + gy[at, part, 4]
                    out[index, part, field] = result

    def couple(at):
        def strip(step, _):
            span = pl.ds(pl.multiple_of(step * 8, 8), 8)
            base = [[bbuf[at, part, which, span, :] for part in range(2)] for which in range(3)]
            for index in range(local):
                source = (first + index + total - at) % total
                for field in range(fields):
                    real = out[index, 0, field, span, :]
                    imag = out[index, 1, field, span, :]
                    for which, values in ((0, gx), (1, gy), (2, pbuf)):
                        a_real, a_imag = base[which]
                        q_real = values[source, 0, field, span, :]
                        q_imag = values[source, 1, field, span, :]
                        real = real + a_real * q_real - a_imag * q_imag
                        imag = imag + a_real * q_imag + a_imag * q_real
                    out[index, 0, field, span, :] = real
                    out[index, 1, field, span, :] = imag
            return 0

        lax.fori_loop(0, rows // 8, strip, 0)

    def wait_y(distance, kind, index):
        for other, what, which, copy in y_copies:
            if (other, what, which) == (distance, kind, index):
                copy.wait_recv()

    slope_y(me)
    for copy in rim_pending[0]:
        copy.wait_recv()
    relay_rims(0)
    slope_x(me)
    own_terms()
    for index in range(local):
        relays[0, 0, index].wait_recv()
    slope_y(partner)
    relays[0].wait_recv()
    slope_x(partner)

    for distance in range(1, chips):
        for index in range(local):
            wait_y(distance, 0, index)
            relay(distance, 0, index)
        pack(distance)
        send_rims(distance)
    for distance in range(1, chips):
        slope_y(group_at(distance, True))
        for index in range(local):
            relays[distance, 0, index].wait_recv()
        slope_y(group_at(distance, False))
    for distance in range(1, chips):
        for index in range(local - 1):
            wait_y(distance, 1, index)
            relay(distance, 1, index)
    for distance in range(1, chips):
        for copy in rim_pending[distance]:
            copy.wait_recv()
        relay_rims(distance)
        slope_x(group_at(distance, True))
    for distance in range(1, chips):
        relays[distance].wait_recv()
        slope_x(group_at(distance, False))

    copy_b.wait()
    for index in range(local):
        couple(first + index)
    for index in range(local):
        relays[0, 1, index].wait_recv()
        couple(partner * local + index)
    for distance in range(1, chips):
        wait_y(distance, 1, local - 1)
        relay(distance, 1, local - 1)
    for distance in range(1, chips):
        for index in range(local):
            couple(group_at(distance, True) * local + index)
    for distance in range(1, chips):
        for index in range(local):
            relays[distance, 1, index].wait_recv()
            couple(group_at(distance, False) * local + index)

    for _, _, _, copy in y_copies:
        copy.wait_send()
    for copies in rim_pending.values():
        for copy in copies:
            copy.wait_send()
    for copy in relays.values():
        copy.wait_send()


def shards(perturbation, base_flow, viscosity):
    local, parts, fields, rows, width = perturbation.shape
    groups = lax.axis_size("harm")
    tiles = lax.axis_size("tile")
    chips = groups // 2
    if chips == 2 and rows % 16 == 0:
        return halves(perturbation, base_flow, viscosity)
    total = local * groups
    rim = -(-(local * parts * fields + 1) // 8) * 8
    kinds = base_flow.shape[2]
    dma = pltpu.SemaphoreType.DMA
    f32 = jnp.float32
    return pl.pallas_call(
        functools.partial(kernel, groups, tiles),
        out_shape=jax.ShapeDtypeStruct(perturbation.shape, f32),
        in_specs=[pl.BlockSpec(memory_space=pl.ANY)] * 3,
        out_specs=pl.BlockSpec(memory_space=pltpu.VMEM),
        scratch_shapes=[
            pltpu.VMEM((total, 2, fields, rows, width), f32),
            pltpu.VMEM((total, 2, kinds, rows, width), f32),
            pltpu.VMEM((rows, width), f32),
            pltpu.VMEM((chips, 2, rim, width), f32),
            pltpu.VMEM((groups, 2, rim, width), f32),
            pltpu.VMEM((total, 2, fields, rows, width), f32),
            pltpu.VMEM((total, 2, fields, rows, width), f32),
            dma((3,)),
            dma((chips - 1, 2, local)),
            dma((chips - 1, 2, local)),
            dma((chips, 2, local)),
            dma((chips, 2, local)),
            dma((chips, 2)),
            dma((chips, 2)),
            dma((chips,)),
            dma((chips,)),
        ],
        compiler_params=pltpu.CompilerParams(collective_id=0, has_side_effects=True),
    )(perturbation, base_flow, viscosity)


def half_kernel(
    groups,
    tiles,
    p_hbm,
    b_hbm,
    v_hbm,
    out_hbm,
    full,
    phalf,
    bhalf,
    vbuf,
    stage,
    inner,
    zrims,
    edges,
    outer,
    fixes,
    fixed,
    kept,
    gx,
    gy,
    total,
    sent,
    back,
    local_sem,
    out_sem,
    y_send,
    y_recv,
    chip_send,
    chip_recv,
    z_send,
    z_recv,
    up_token,
    down_token,
):
    local, _, fields, rows, width = p_hbm.shape
    harmonics = phalf.shape[0]
    half = rows // 2
    rim_rows = local * 2 * fields
    rim = stage.shape[1]
    me = lax.axis_index("harm")
    chip, core = me // 2, me % 2
    place = lax.axis_index("tile")
    partner = chip * 2 + (1 - core)
    across = (1 - chip) * 2 + core
    corner = (1 - chip) * 2 + (1 - core)
    above, below = (place + 1) % tiles, (place + tiles - 1) % tiles
    first = me * local
    mine = pl.ds(pl.multiple_of(chip * half, 8), half)
    theirs = pl.ds(pl.multiple_of((1 - chip) * half, 8), half)

    def at_group(ref, group):
        return ref.at[pl.ds(group * local, local)]

    loads = [
        pltpu.make_async_copy(source, dest, local_sem.at[at])
        for at, (source, dest) in enumerate(
            (
                (p_hbm, full),
                (v_hbm, vbuf),
                (p_hbm.at[:, :, :, mine, :], at_group(phalf, me)),
                (b_hbm.at[:, :, :, mine, :], at_group(bhalf, me)),
            )
        )
    ]
    for copy in loads:
        copy.start()

    barrier = pltpu.get_barrier_semaphore()
    pl.semaphore_signal(barrier, inc=1, device_id={"harm": across}, device_id_type=MESH)
    pl.semaphore_signal(barrier, inc=1, device_id={"harm": partner}, device_id_type=MESH)

    @pl.when(place < tiles - 1)
    def _():
        pl.semaphore_signal(barrier, inc=1, device_id={"tile": above}, device_id_type=MESH)

    @pl.when(place > 0)
    def _():
        pl.semaphore_signal(barrier, inc=1, device_id={"tile": below}, device_id_type=MESH)

    in_line = (place < tiles - 1).astype(jnp.int32) + (place > 0).astype(jnp.int32)

    loads[0].wait()
    loads[1].wait()
    for index in range(local):
        for part in range(2):
            for field in range(fields):
                row = (index * 2 + part) * fields + field
                span = slice(row, row + 1)
                stage[0, span, :] = full[index, part, field, 0:1, :]
                stage[1, span, :] = full[index, part, field, rows - 1 : rows, :]
                edges[me, span, :] = full[index, part, field, pl.ds(half - chip, 1), :]
                inner[span, :] = full[index, part, field, pl.ds(half - 1 + chip, 1), :]
    stage[0, rim_rows : rim_rows + 1, :] = vbuf[0:1, :]
    stage[1, rim_rows : rim_rows + 1, :] = vbuf[rows - 1 : rows, :]

    pl.semaphore_wait(barrier, 2 + in_line)

    started = []

    def remote(source, dest, send, recv, at, **device):
        copy = pltpu.make_async_remote_copy(
            src_ref=source,
            dst_ref=dest,
            send_sem=send.at[at],
            recv_sem=recv.at[at],
            device_id=device,
            device_id_type=MESH,
        )
        copy.start()
        started.append(copy)
        return copy

    def over_y(source, dest, at):
        return remote(source, dest, y_send, y_recv, at, harm=across)

    def on_chip(source, dest, at):
        return remote(source, dest, chip_send, chip_recv, at, harm=partner)

    def send_field(field):
        return over_y(
            p_hbm.at[:, :, field, theirs, :], at_group(phalf, me).at[:, :, field], 3 + field
        )

    y_base = over_y(b_hbm.at[:, :, :, theirs, :], at_group(bhalf, me), 0)
    y_inner = over_y(inner, edges.at[me], 2)
    y_field = [send_field(field) for field in range(fields)]
    c_base = on_chip(b_hbm.at[:, :, :, mine, :], at_group(bhalf, me), 0)
    c_own = on_chip(p_hbm.at[:, :, :, mine, :], at_group(phalf, me), 1)
    c_edges = on_chip(edges.at[me], edges.at[me], 2)

    if tiles > 2:

        @pl.when(place >= 2)
        def _():
            pl.semaphore_wait(up_token, 1)

        @pl.when((place >= 1) & (place < tiles - 1))
        def _():
            pl.semaphore_signal(up_token, inc=1, device_id={"tile": above}, device_id_type=MESH)

        @pl.when(place <= tiles - 3)
        def _():
            pl.semaphore_wait(down_token, 1)

        @pl.when((place >= 1) & (place < tiles - 1))
        def _():
            pl.semaphore_signal(down_token, inc=1, device_id={"tile": below}, device_id_type=MESH)

    z_rims = [
        remote(stage.at[0], zrims.at[0], z_send, z_recv, 1, tile=below),
        remote(stage.at[1], zrims.at[1], z_send, z_recv, 0, tile=above),
    ]

    row_at = lax.broadcasted_iota(jnp.int32, (rows, width), 0)

    def neighbours(value, high, low):
        count = value.shape[0]
        row = row_at[:count]
        east = jnp.where(row == count - 1, high, pltpu.roll(value, count - 1, 0))
        west = jnp.where(row == 0, low, pltpu.roll(value, 1, 0))
        return east, west

    def north(value):
        return pltpu.roll(value, width - 1, 1)

    def south(value):
        return pltpu.roll(value, 1, 1)

    def slopes(group, field):
        for index in range(local):
            at = group * local + index
            for part in range(2):
                row = (index * 2 + part) * fields + field
                value = phalf[at, part, field]
                inside = edges[group, row : row + 1, :]
                east, west = neighbours(
                    value, inside * (1 - chip).astype(inside.dtype), inside * chip.astype(inside.dtype)
                )
                gx[at, part, field] = 0.5 * (east - west)
                gy[at, part, field] = 0.5 * (north(value) - south(value))

    def own_terms():
        center = vbuf[...]
        east, west = neighbours(
            center,
            zrims[0, rim_rows : rim_rows + 1, :],
            zrims[1, rim_rows : rim_rows + 1, :],
        )
        east_face = 0.5 * (center + east)
        west_face = 0.5 * (center + west)
        north_face = 0.5 * (center + north(center))
        south_face = 0.5 * (center + south(center))
        for index in range(local):
            at = first + index
            signed = jnp.where(at < harmonics // 2, at, at - harmonics)
            frequency = omega_base * signed.astype(jnp.float32)
            for part in range(2):

                def sides(field):
                    row = (index * 2 + part) * fields + field
                    return neighbours(
                        full[index, part, field],
                        zrims[0, row : row + 1, :],
                        zrims[1, row : row + 1, :],
                    )

                def along_x(field):
                    up, down = sides(field)
                    return 0.5 * (up - down)

                def along_y(field):
                    value = full[index, part, field]
                    return 0.5 * (north(value) - south(value))

                dilation = along_x(1) + along_y(2)
                sound = {0: dilation, 4: dilation, 1: along_x(4), 2: along_y(4)}
                for field in range(fields):
                    value = full[index, part, field]
                    up, down = sides(field)
                    damping = (
                        east_face * (up - value)
                        - west_face * (value - down)
                        + north_face * (north(value) - value)
                        - south_face * (value - south(value))
                    )
                    turned = full[index, 1 - part, field] * frequency
                    result = turned if part else -turned
                    if field in sound:
                        result = result + sound[field]
                    total[index, part, field] = result - damping

    y_base.wait_recv()
    c_base_across = on_chip(at_group(bhalf, across), at_group(bhalf, across), 3)
    loads[2].wait()
    loads[3].wait()
    for field in range(fields):
        slopes(me, field)

    c_field = []

    def relay_field(field):
        y_field[field].wait_recv()
        c_field.append(
            on_chip(
                at_group(phalf, across).at[:, :, field],
                at_group(phalf, across).at[:, :, field],
                5 + field,
            )
        )

    relay_field(0)
    c_own.wait_recv()
    c_edges.wait_recv()
    for field in range(fields):
        slopes(partner, field)
    z_rims[0].wait_recv()
    z_rims[1].wait_recv()
    y_outer = over_y(zrims.at[chip], outer.at[me], 1)
    c_outer = on_chip(zrims.at[1 - chip], outer.at[me], 5 + fields)
    outer[me] = zrims[1 - chip]
    y_inner.wait_recv()
    c_edges_across = on_chip(edges.at[across], edges.at[across], 4)
    c_base.wait_recv()
    c_base_across.wait_recv()
    if fields > 1:
        relay_field(1)

    targets = [first + index for index in range(local)]
    targets += [across * local + index for index in range(local)]

    def couple(field):
        def step(source, sums):
            moved = [
                [values[source, part, field] for part in range(2)] for values in (gx, gy, phalf)
            ]
            after = []
            for number, target in enumerate(targets):
                real, imag = sums[2 * number], sums[2 * number + 1]
                at = (target + harmonics - source) % harmonics
                for which in range(3):
                    a_real, a_imag = bhalf[at, 0, which], bhalf[at, 1, which]
                    q_real, q_imag = moved[which]
                    real = real + a_real * q_real - a_imag * q_imag
                    imag = imag + a_real * q_imag + a_imag * q_real
                after += [real, imag]
            return tuple(after)

        zero = jnp.zeros((half, width), jnp.float32)
        sums = lax.fori_loop(0, harmonics, step, (zero,) * (4 * local), unroll=8)
        for index in range(local):
            for part in range(2):
                sent[index, part, field] = sums[2 * (local + index) + part]
        for index in range(local):
            for part in range(2):
                kept[index, part, field] = sums[2 * index + part]

    def fix():
        edge = chip * (half - 1)
        sign = 0.5 * (2 * chip - 1).astype(jnp.float32)
        for number, target in enumerate(targets):
            real = jnp.zeros((fields, width), jnp.float32)
            imag = real
            for group in (me, partner, across, corner):
                for index in range(local):
                    at = (target + harmonics - group * local - index) % harmonics
                    a_real = sign * bhalf[at, 0, 0, pl.ds(edge, 1), :]
                    a_imag = sign * bhalf[at, 1, 0, pl.ds(edge, 1), :]
                    row = index * 2 * fields
                    q_real = outer[group, row : row + fields, :]
                    q_imag = outer[group, row + fields : row + 2 * fields, :]
                    real = real + a_real * q_real - a_imag * q_imag
                    imag = imag + a_real * q_imag + a_imag * q_real
            row = number // local * rim + number % local * 2 * fields
            fixes[row : row + fields, :] = real
            fixes[row + fields : row + 2 * fields, :] = imag

    def put(span, which):
        copy = pltpu.make_async_copy(
            total.at[:, :, :, span, :], out_hbm.at[:, :, :, span, :], out_sem.at[which]
        )
        copy.start()
        puts.append(copy)

    puts = []
    y_back = []
    for field in range(fields):
        slopes(across, field)
        if field == 0:
            c_edges_across.wait_recv()
        c_field[field].wait_recv()
        slopes(corner, field)
        couple(field)
        y_back.append(over_y(sent.at[:, :, field], back.at[:, :, field], 3 + fields + field))
        if field + 2 < fields:
            relay_field(field + 2)
        if field == 2:
            own_terms()
        if field == min(2, fields - 1):
            y_outer.wait_recv()
            c_outer_across = on_chip(outer.at[across], outer.at[across], 6 + fields)

    c_outer.wait_recv()
    c_outer_across.wait_recv()
    fix()
    y_fix = over_y(fixes.at[rim : 2 * rim], fixed, 3 + 2 * fields)

    def add_rows(rows_ref, at):
        for index in range(local):
            for part in range(2):
                for field in range(fields):
                    row = (index * 2 + part) * fields + field
                    total[index, part, field, pl.ds(at, 1), :] += rows_ref[row : row + 1, :]

    for field in range(fields):
        for index in range(local):
            for part in range(2):
                total[index, part, field, mine, :] += kept[index, part, field]
    add_rows(fixes, chip * (rows - 1))
    put(mine, 0)

    for field in range(fields):
        y_back[field].wait_recv()
        for index in range(local):
            for part in range(2):
                total[index, part, field, theirs, :] += back[index, part, field]
    y_fix.wait_recv()
    add_rows(fixed, (1 - chip) * (rows - 1))
    put(theirs, 1)

    for copy in started:
        copy.wait_send()
    for copy in puts:
        copy.wait()


def halves(perturbation, base_flow, viscosity):
    local, _, fields, rows, width = perturbation.shape
    groups = lax.axis_size("harm")
    tiles = lax.axis_size("tile")
    harmonics = local * groups
    half = rows // 2
    rim = -(-(local * 2 * fields + 1) // 8) * 8
    kinds = base_flow.shape[2]
    dma = pltpu.SemaphoreType.DMA
    f32 = jnp.float32
    return pl.pallas_call(
        functools.partial(half_kernel, groups, tiles),
        out_shape=jax.ShapeDtypeStruct(perturbation.shape, f32),
        in_specs=[pl.BlockSpec(memory_space=pl.ANY)] * 3,
        out_specs=pl.BlockSpec(memory_space=pl.ANY),
        scratch_shapes=[
            pltpu.VMEM((local, 2, fields, rows, width), f32),
            pltpu.VMEM((harmonics, 2, fields, half, width), f32),
            pltpu.VMEM((harmonics, 2, kinds, half, width), f32),
            pltpu.VMEM((rows, width), f32),
            pltpu.VMEM((2, rim, width), f32),
            pltpu.VMEM((rim, width), f32),
            pltpu.VMEM((2, rim, width), f32),
            pltpu.VMEM((groups, rim, width), f32),
            pltpu.VMEM((groups, rim, width), f32),
            pltpu.VMEM((2 * rim, width), f32),
            pltpu.VMEM((rim, width), f32),
            pltpu.VMEM((local, 2, fields, half, width), f32),
            pltpu.VMEM((harmonics, 2, fields, half, width), f32),
            pltpu.VMEM((harmonics, 2, fields, half, width), f32),
            pltpu.VMEM((local, 2, fields, rows, width), f32),
            pltpu.VMEM((local, 2, fields, half, width), f32),
            pltpu.VMEM((local, 2, fields, half, width), f32),
            dma((4,)),
            dma((2,)),
            dma((4 + 2 * fields,)),
            dma((4 + 2 * fields,)),
            dma((7 + fields,)),
            dma((7 + fields,)),
            dma((2,)),
            dma((2,)),
            pltpu.SemaphoreType.REGULAR,
            pltpu.SemaphoreType.REGULAR,
        ],
        compiler_params=pltpu.CompilerParams(collective_id=0, has_side_effects=True),
    )(perturbation, base_flow, viscosity)


def solution(mesh):
    placed = (
        P("harm", None, None, ("parts", "tile"), None),
        P("harm", None, None, ("parts", "tile"), None),
        P(("parts", "tile"), None),
    )
    return jax.shard_map(
        shards,
        mesh=mesh,
        in_specs=placed,
        out_specs=P("harm", None, None, ("parts", "tile"), None),
        check_vma=False,
    )
```
